32 devices in a mesh: tm: 8 (over z, core), net: 4 (over y, x).
Axes of the slice: x: 2, y: 2, z: 4, core: 2. Of those that a mesh axis runs over, the one named last changes fastest.
Arguments:
- ptdf: bfloat16 [16384, 4096], P('net'), may hold values from -0.09375 to 0.09375
- demand: float32 [4096, 512], P('net', 'tm'), may hold values from 0 to 2
- generation: float32 [4096, 512], P('net', 'tm'), may hold values from 0 to 2
- cost: float32 [4096, 512], P('net', 'tm'), may hold values from 0.2 to 4
- gen_cap: float32 [4096], P('net'), may hold values from 0.5 to 4
- storage: float32 [2048, 512], P('net', 'tm'), may hold values from -3 to 3
- wear: float32 [2048], P('net'), may hold values from 0.1 to 2
- initial_charge: float32 [2048], P('net'), may hold values from 0 to 2
- leakage: float32 [2048], P('net'), may hold values from 0.0005859375 to 0.05
- line_dual: float32 [16384, 512], P('net', 'tm'), may hold values from -3 to 3
- line_index: int32 [16384], P('net'), may hold values from 0 to 4095
- rating: float32 [4096], replicated, may hold values from 0.3 to 3
- storage_bus: int32 [2048], replicated, may hold values from 0 to 4095
- balance_dual: float32 [512], P('tm'), may hold values from -4 to 4
- hour_block: int32 [512], P('tm'), may hold values from 0 to 23
- block_price: float32 [24], replicated, may hold values from -4 to 4
Outputs:
- generation_next: float32 [4096, 512], P('net', 'tm')
- storage_next: float32 [2048, 512], P('net', 'tm')
- charge: float32 [2048, 512], P('net', 'tm')
- line_dual_next: float32 [16384, 512], P('net', 'tm')
- balance_price: float32 [512], P('tm')
The draws below stay inside these ranges and needn't reach their ends.
All inputs are finite; a program needn't handle non-finite values.
Results may differ from the reference program's by a relative error of at most 0.0028.
Values may be sent and summed in bfloat16 or wider, within the bound.
A program may use at most 128 MiB of HBM per device.

```python
import math
import jax
import jax.numpy as jnp
from jax import lax

NB = 4096
L = 16384
S = 2048
LINES = 4096
BLOCKS = 24
PASSES = 2
H = 512


def plant(array, key, least, largest):
    place = [jax.random.randint(jax.random.fold_in(key, axis), (), 0, length) for axis, length in enumerate(array.shape)]
    longest = array.shape.index(max(array.shape))
    neighbour = place[:longest] + [(place[longest] + 1) % array.shape[longest]] + place[longest + 1:]
    return array.at[tuple(place)].set(least).at[tuple(neighbour)].set(largest)


def block_levels(stream_key, dims, cuts, least, top_value):
    def one(dim, blocks):
        heights = jax.random.uniform(jax.random.fold_in(jax.random.fold_in(stream_key, 6), dim), (blocks,), jnp.float32, least / len(cuts), top_value / len(cuts))
        return jnp.repeat(jnp.exp(heights), dims[dim] // blocks).reshape((-1,) + (1,) * (len(dims) - dim - 1))

    gain = one(*cuts[0])
    for cut in cuts[1:]:
        gain = gain * one(*cut)
    return gain


def centred(key, dims, scale, most, cuts=(), dtype=jnp.bfloat16):
    factor_of = block_levels(key, dims, cuts, -0.22, 0.18) if cuts else 1.0
    array = jax.random.normal(key, dims, jnp.float32) * scale * factor_of
    return jnp.minimum(jnp.maximum(array, -most), most).astype(dtype)


def setup_inputs(seed: int = 0) -> dict:
    key_list = jax.random.split(jax.random.key(seed), 17)
    ptdf = centred(key_list[0], (L, NB), NB ** -0.5, 0.09375, ((0, 4),))
    demand = jnp.clip(2.0 * jax.random.uniform(key_list[1], (NB, H), jnp.float32) ** block_levels(key_list[1], (NB, H), ((0, 4), (1, 8)), -0.2, 0.2), 0.0, 2.0)
    generation = jnp.clip(2.0 * jax.random.uniform(key_list[2], (NB, H), jnp.float32) ** block_levels(key_list[2], (NB, H), ((0, 4), (1, 8)), -0.2, 0.2), 0.0, 2.0)
    cost = jnp.clip(jnp.exp(math.log(4.0) - 2.9957323 * jax.random.uniform(key_list[3], (NB, H), jnp.float32) ** block_levels(key_list[3], (NB, H), ((0, 4), (1, 8)), -0.2, 0.2)), 0.2, 4.0)
    gen_cap = jnp.clip(jnp.exp(math.log(4.0) - 2.0794415 * jax.random.uniform(key_list[4], (NB,), jnp.float32) ** block_levels(key_list[4], (NB,), ((0, 4),), -0.2, 0.2)), 0.5, 4.0)
    storage = centred(key_list[5], (S, H), 0.5, 3.0, ((0, 4), (1, 8)), jnp.float32)
    wear = jnp.clip(jnp.exp(math.log(2.0) - 2.9957323 * jax.random.uniform(key_list[6], (S,), jnp.float32) ** block_levels(key_list[6], (S,), ((0, 4),), -0.2, 0.2)), 0.1, 2.0)
    initial_charge = jnp.clip(2.0 * jax.random.uniform(key_list[7], (S,), jnp.float32) ** block_levels(key_list[7], (S,), ((0, 4),), -0.2, 0.2), 0.0, 2.0)
    leakage = jnp.clip(jnp.exp(math.log(0.05) - 4.446565 * jax.random.uniform(key_list[8], (S,), jnp.float32) ** block_levels(key_list[8], (S,), ((0, 4),), -0.2, 0.2)), 0.0005859375, 0.05)
    line_dual = centred(key_list[9], (L, H), 0.3, 3.0, ((0, 4), (1, 8)), jnp.float32)
    line_index = plant(jax.random.randint(key_list[10], (L,), 0, LINES), jax.random.fold_in(key_list[10], 1), 0, LINES - 1).astype(jnp.int32)
    rating = jnp.clip(jnp.exp(jax.random.uniform(key_list[11], (LINES,), jnp.float32, math.log(0.3), math.log(3.0))), 0.3, 3.0)
    storage_bus = plant(jax.random.randint(key_list[12], (S,), 0, NB), jax.random.fold_in(key_list[12], 1), 0, NB - 1).astype(jnp.int32)
    balance_dual = centred(key_list[13], (H,), 1.0, 4.0, ((0, 8),), jnp.float32)
    hour_block = plant(jax.random.randint(key_list[14], (H,), 0, BLOCKS), jax.random.fold_in(key_list[14], 1), 0, BLOCKS - 1).astype(jnp.int32)
    block_price = centred(key_list[15], (BLOCKS,), 1.0, 4.0, (), jnp.float32)
    return {"ptdf": ptdf, "demand": demand, "generation": generation, "cost": cost, "gen_cap": gen_cap, "storage": storage, "wear": wear, "initial_charge": initial_charge, "leakage": leakage, "line_dual": line_dual, "line_index": line_index, "rating": rating, "storage_bus": storage_bus, "balance_dual": balance_dual, "hour_block": hour_block, "block_price": block_price}


STEP = 0.1
BAL = 0.5
STEP_UNIT = 0.2
ETA = 0.0625


def product(left, right):
    return jnp.dot(left.astype(jnp.float32), right.astype(jnp.float32), precision=lax.Precision.HIGHEST)


def reference(ptdf, demand, generation, cost, gen_cap, storage, wear, initial_charge, leakage, line_dual, line_index, rating, storage_bus, balance_dual, hour_block, block_price):
    limit = rating[line_index][:, None]
    unit_columns = ptdf[:, storage_bus]
    unit_flow = product(unit_columns, storage.astype(jnp.bfloat16))
    unit_total = jnp.sum(storage, axis=0)
    gen = generation
    dual = line_dual
    price = balance_dual
    for turn in range(PASSES):
        injection = (gen - demand).astype(jnp.bfloat16)
        flows = product(ptdf, injection) + unit_flow
        shifted = flows + dual
        dual = shifted - jnp.clip(shifted, -limit, limit)
        pull = product(ptdf.T, dual.astype(jnp.bfloat16))
        trial = jnp.clip(gen - STEP * (cost - price[None, :] + pull), 0.0, gen_cap[:, None])
        mismatch = jnp.sum(trial - demand, axis=0) + unit_total
        gen = trial - mismatch[None, :] / NB
        price = price - BAL * mismatch / NB
    hour_price = block_price[hour_block]
    storage_next = jnp.clip(storage + STEP_UNIT * (price[None, :] + hour_price[None, :] - wear[:, None] * storage), -1.0, 1.0)
    keep = 1.0 - leakage

    def advance(carry, column):
        carry = keep * carry - ETA * column
        return carry, carry

    _, charge = lax.scan(advance, initial_charge, storage_next.T)
    return gen, storage_next, charge.T, dual, price
```

```python
import functools

import jax
import jax.numpy as jnp
from jax import lax
from jax.experimental import pallas as pl
from jax.experimental.pallas import tpu as pltpu
from jax.sharding import PartitionSpec as P

PASSES = 2
STEP = 0.1
BAL = 0.5
STEP_UNIT = 0.2
ETA = 0.0625
MESH = pl.DeviceIdType.MESH
NT = (((1,), (1,)), ((), ()))
NN = (((1,), (0,)), ((), ()))


def partner(me, step, count):
    if count & (count - 1):
        return lax.rem(me + step, count)
    other, bit = 0, 1
    while bit < count:
        mine = lax.rem(me // bit, 2)
        other = other + bit * ((1 - mine) if step & bit else mine)
        bit *= 2
    return other


def source(me, step, count):
    if count & (count - 1):
        return lax.rem(me + count - step, count)
    return partner(me, step, count)


def as_row(col):
    n = col.shape[0]
    eye = lax.broadcasted_iota(jnp.int32, (n, n), 0) == lax.broadcasted_iota(jnp.int32, (n, n), 1)
    return jnp.sum(jnp.where(eye, col, 0), axis=0, keepdims=True)


def as_col(row):
    n = row.shape[1]
    eye = lax.broadcasted_iota(jnp.int32, (n, n), 0) == lax.broadcasted_iota(jnp.int32, (n, n), 1)
    return jnp.sum(jnp.where(eye, row, 0), axis=1, keepdims=True)


def kernel(
    nets,
    spans,
    buses,
    ptdf_hbm,
    demand,
    generation,
    cost,
    cap,
    storage,
    wear,
    initial,
    leakage,
    line_dual,
    line_index,
    rating,
    storage_bus,
    price_in,
    hour_block,
    block_price,
    gen_out,
    storage_out,
    charge_out,
    dual_out,
    price_out,
    ptdf,
    units,
    unit_cols,
    inj,
    acc,
    dual_half,
    part_send,
    part_recv,
    limit,
    sums,
    lasts,
    load_sem,
    unit_sem,
    inj_sem,
    part_sem,
    sum_sem,
    last_sem,
):
    f32, bf16 = jnp.float32, jnp.bfloat16
    me = lax.axis_index("net")
    place = lax.axis_index("tm")
    hours, nb = demand.shape
    rows = line_dual.shape[1]
    total_units = storage_bus.shape[1]
    su = storage.shape[1]

    def load(j):
        owner = source(me, j, nets)
        cols = pl.ds(pl.multiple_of(owner * nb, nb), nb)
        return pltpu.make_async_copy(ptdf_hbm.at[:, cols], ptdf.at[:, cols], load_sem.at[j])

    for j in range(nets):
        load(j).start()

    barrier = pltpu.get_barrier_semaphore()
    for step in range(1, nets):
        pl.semaphore_signal(
            barrier, inc=1, device_id={"net": partner(me, step, nets)}, device_id_type=MESH
        )
    for step in range(1, spans):
        pl.semaphore_signal(
            barrier, inc=1, device_id={"tm": lax.rem(place + step, spans)}, device_id_type=MESH
        )

    units[0] = storage[...].astype(bf16)
    inj[0, 0] = (generation[...] - demand[...]).astype(bf16)
    pl.semaphore_wait(barrier, nets - 1 + spans - 1)

    pending = []

    def send(src, dst, sems, step, axis="net"):
        if axis == "net":
            target = {"net": partner(me, step, nets)}
        else:
            target = {"tm": lax.rem(place + step, spans)}
        copy = pltpu.make_async_remote_copy(
            src_ref=src,
            dst_ref=dst,
            send_sem=sems.at[0, step],
            recv_sem=sems.at[1, step],
            device_id=target,
            device_id_type=MESH,
        )
        copy.start()
        pending.append(copy)
        return copy

    unit_copies = [send(units.at[0], units.at[s], unit_sem, s) for s in range(1, nets)]
    inj_copies = [send(inj.at[0, 0], inj.at[0, s], inj_sem.at[0], s) for s in range(1, nets)]

    index = line_index[...]
    lane, group = lax.rem(index, 128), index // 128
    found = jnp.zeros(index.shape, f32)
    for q in range(rating.shape[0]):
        row = jnp.broadcast_to(rating[q : q + 1, :], index.shape)
        found = jnp.where(
            group == q,
            jnp.take_along_axis(row, lane, axis=1, mode="promise_in_bounds"),
            found,
        )
    limit[...] = found

    unit_part = jnp.sum(storage[...], axis=1, keepdims=True)
    price = as_col(price_in[...])
    block = as_col(hour_block[...])
    kinds = block_price.shape[1]
    hour_price = jnp.sum(
        jnp.where(
            block == lax.broadcasted_iota(jnp.int32, (hours, kinds), 1), block_price[...], 0.0
        ),
        axis=1,
        keepdims=True,
    )

    for copy in unit_copies:
        copy.wait_recv()
    ub = min(256, nb)
    for j in range(nets):
        owner = source(me, j, nets)
        base = owner * nb

        def collect(i, c, j=j, base=base):
            bus = base + i * ub + lax.broadcasted_iota(jnp.int32, (ub, su), 0)
            total = jnp.zeros((hours, ub), f32)
            for k in range(nets):
                first = pl.multiple_of(source(me, k, nets) * su, su)
                hit = jnp.where(storage_bus[:, pl.ds(first, su)] == bus, 1.0, 0.0).astype(bf16)
                total = total + lax.dot_general(units[k], hit, NT, preferred_element_type=f32)
            high = total.astype(bf16)
            low = (total - high.astype(f32)).astype(bf16)
            unit_cols[j, :, pl.ds(pl.multiple_of(i * ub, ub), ub)] = jnp.concatenate(
                [high, low], axis=0
            )
            return c

        lax.fori_loop(0, nb // ub, collect, 0)

    rb = min(512, rows)
    cb = min(512, nb)
    gen = None
    for turn in range(PASSES):
        last_j = nets - 1
        for j in range(nets):
            if turn == 0:
                load(j).wait()
            if j > 0:
                inj_copies[j - 1].wait_recv()
            owner = source(me, j, nets)
            cols = pl.ds(pl.multiple_of(owner * nb, nb), nb)

            def flow(i, c, j=j, cols=cols):
                r = pl.ds(pl.multiple_of(i * rb, rb), rb)
                if turn == 0:
                    left = jnp.concatenate([inj[turn, j], unit_cols[j]], axis=0)
                    got = lax.dot_general(left, ptdf[r, cols], NT, preferred_element_type=f32)
                    unit = got[hours : 2 * hours] + got[2 * hours :]
                    got = got[:hours] + unit
                    if j == 0:
                        acc[1, :, r] = unit
                    else:
                        acc[1, :, r] = acc[1, :, r] + unit
                    old = line_dual
                else:
                    got = lax.dot_general(
                        inj[turn, j], ptdf[r, cols], NT, preferred_element_type=f32
                    )
                    if j == 0:
                        got = got + acc[1, :, r]
                    old = dual_out
                if j > 0:
                    got = got + acc[0, :, r]
                if j < last_j:
                    acc[0, :, r] = got
                else:
                    shifted = got + old[:, r]
                    pieces = []
                    for k in range(rb // 128):
                        bound = limit[pl.ds(i * (rb // 128) + k, 1), :]
                        x = shifted[:, k * 128 : (k + 1) * 128]
                        pieces.append(x - jnp.clip(x, -bound, bound))
                    dual = jnp.concatenate(pieces, axis=1)
                    dual_out[:, r] = dual
                    dual_half[:, r] = dual.astype(bf16)
                return c

            lax.fori_loop(0, rows // rb, flow, 0)

        part_copies = []
        for j in list(range(nets - 1, 0, -1)) + [0]:
            owner = partner(me, j, nets)

            def pull_part(i, c, j=j, owner=owner):
                here = pl.ds(pl.multiple_of(i * cb, cb), cb)
                cols = pl.ds(pl.multiple_of(owner * nb + i * cb, cb), cb)
                got = lax.dot_general(
                    dual_half[...], ptdf[:, cols], NN, preferred_element_type=f32
                )
                if j > 0:
                    part_send[turn, j, :, here] = got.astype(bf16)
                else:
                    acc[0, :, here] = got
                return c

            lax.fori_loop(0, nb // cb, pull_part, 0)
            if j > 0:
                part_copies.append(
                    send(part_send.at[turn, j], part_recv.at[turn, j], part_sem.at[turn], j)
                )
        pull = acc[0, :, :nb]
        for step in range(nets - 1, 0, -1):
            part_copies[nets - 1 - step].wait_recv()
            pull = pull + part_recv[turn, step].astype(f32)
        if turn == 0:
            gen = generation[...]
        else:
            gen = gen_out[...]
        trial = jnp.clip(gen - STEP * (cost[...] - price + pull), 0.0, cap[...])
        part = jnp.sum(trial - demand[...], axis=1, keepdims=True) + unit_part
        sums[turn, 0, :, :hours] = jnp.broadcast_to(as_row(part), (8, hours))
        sum_copies = [
            send(sums.at[turn, 0], sums.at[turn, s], sum_sem.at[turn], s) for s in range(1, nets)
        ]
        whole = sums[turn, 0]
        for s in range(1, nets):
            sum_copies[s - 1].wait_recv()
            whole = whole + sums[turn, s]
        mismatch = as_col(whole[0:1, :hours])
        gen = trial - mismatch / buses
        price = price - BAL * mismatch / buses
        gen_out[...] = gen
        if turn + 1 < PASSES:
            inj[turn + 1, 0] = (gen - demand[...]).astype(bf16)
            inj_copies = [
                send(inj.at[turn + 1, 0], inj.at[turn + 1, s], inj_sem.at[turn + 1], s)
                for s in range(1, nets)
            ]

    stored = storage[...]
    stored = jnp.clip(
        stored + STEP_UNIT * (price + hour_price - wear[...] * stored), -1.0, 1.0
    )
    storage_out[...] = stored
    keep = 1.0 - leakage[...]
    running = -ETA * stored
    hour = lax.broadcasted_iota(jnp.int32, (hours, su), 0)
    growth = jnp.ones((hours, su), f32)
    factor = keep
    span = 1
    while span < hours:
        moved = jnp.where(hour >= span, pltpu.roll(running, span, axis=0), 0.0)
        running = running + factor * moved
        growth = jnp.where(lax.rem((hour + 1) // span, 2) == 1, growth * factor, growth)
        factor = factor * factor
        span = span * 2
    while span <= hours:
        growth = jnp.where(lax.rem((hour + 1) // span, 2) == 1, growth * factor, growth)
        factor = factor * factor
        span = span * 2
    lasts[0] = jnp.broadcast_to(running[hours - 1 :, :], (8, su))
    last_copies = [
        send(lasts.at[0], lasts.at[s], last_sem, s, "tm") for s in range(1, spans)
    ]
    price_out[...] = as_row(price)
    block_keep = growth[hours - 1 :, :]
    for copy in last_copies:
        copy.wait_recv()
    entering = initial[...]
    for s in range(spans - 1, 0, -1):
        entering = jnp.where(s <= place, block_keep * entering + lasts[s, 0:1, :], entering)
    charge_out[...] = growth * entering + running
    for copy in pending:
        copy.wait_send()


def per_device(
    ptdf,
    demand,
    generation,
    cost,
    gen_cap,
    storage,
    wear,
    initial_charge,
    leakage,
    line_dual,
    line_index,
    rating,
    storage_bus,
    balance_dual,
    hour_block,
    block_price,
):
    nets, spans = lax.axis_size("net"), lax.axis_size("tm")
    rows, _ = ptdf.shape
    nb, hours = demand.shape
    su = storage.shape[0]
    buses = nb * nets
    f32, bf16 = jnp.float32, jnp.bfloat16
    vmem = pl.BlockSpec(memory_space=pltpu.VMEM)
    sem = pltpu.SemaphoreType.DMA
    gen, stored, charge, dual, price = pl.pallas_call(
        functools.partial(kernel, nets, spans, buses),
        out_shape=(
            jax.ShapeDtypeStruct((hours, nb), f32),
            jax.ShapeDtypeStruct((hours, su), f32),
            jax.ShapeDtypeStruct((hours, su), f32),
            jax.ShapeDtypeStruct((hours, rows), f32),
            jax.ShapeDtypeStruct((1, hours), f32),
        ),
        in_specs=[pl.BlockSpec(memory_space=pl.ANY)] + [vmem] * 15,
        out_specs=(vmem,) * 5,
        scratch_shapes=[
            pltpu.VMEM(ptdf.shape, bf16),
            pltpu.VMEM((nets, hours, su), bf16),
            pltpu.VMEM((nets, 2 * hours, nb), bf16),
            pltpu.VMEM((PASSES, nets, hours, nb), bf16),
            pltpu.VMEM((2, hours, max(rows, nb)), f32),
            pltpu.VMEM((hours, rows), bf16),
            pltpu.VMEM((PASSES, nets, hours, nb), bf16),
            pltpu.VMEM((PASSES, nets, hours, nb), bf16),
            pltpu.VMEM((rows // 128, 128), f32),
            pltpu.VMEM((PASSES, nets, 8, 128), f32),
            pltpu.VMEM((spans, 8, su), f32),
            sem((nets,)),
            sem((2, nets)),
            sem((PASSES, 2, nets)),
            sem((PASSES, 2, nets)),
            sem((PASSES, 2, nets)),
            sem((2, spans)),
        ],
        compiler_params=pltpu.CompilerParams(
            collective_id=0, has_side_effects=True, vmem_limit_bytes=64 * 1000 * 1000
        ),
    )(
        ptdf,
        demand.T,
        generation.T,
        cost.T,
        gen_cap[None, :],
        storage.T,
        wear[None, :],
        initial_charge[None, :],
        leakage[None, :],
        line_dual.T,
        line_index.reshape(-1, 128),
        rating.reshape(-1, 128),
        storage_bus[None, :],
        balance_dual[None, :],
        hour_block[None, :],
        block_price[None, :],
    )
    return (gen.T, stored.T, charge.T, dual.T, price[0])


def solution(mesh):
    in_specs = (
        P("net", None),
        P("net", "tm"),
        P("net", "tm"),
        P("net", "tm"),
        P("net"),
        P("net", "tm"),
        P("net"),
        P("net"),
        P("net"),
        P("net", "tm"),
        P("net"),
        P(),
        P(),
        P("tm"),
        P("tm"),
        P(),
    )
    out_specs = (P("net", "tm"), P("net", "tm"), P("net", "tm"), P("net", "tm"), P("tm"))
    return jax.shard_map(
        per_device, mesh=mesh, in_specs=in_specs, out_specs=out_specs, check_vma=False
    )
```

```python
import functools

import jax
import jax.numpy as jnp
from jax import lax
from jax.experimental import pallas as pl
from jax.experimental.pallas import tpu as pltpu
from jax.sharding import PartitionSpec as P

PASSES = 2
STEP = 0.1
BAL = 0.5
STEP_UNIT = 0.2
ETA = 0.0625
MESH = pl.DeviceIdType.MESH
NT = (((1,), (1,)), ((), ()))
NN = (((1,), (0,)), ((), ()))


def peer(me, step, count):
    other, bit = 0, 1
    while bit < count:
        mine = lax.rem(me // bit, 2)
        other = other + bit * ((1 - mine) if step & bit else mine)
        bit *= 2
    return other


def as_row(col):
    n = col.shape[0]
    eye = lax.broadcasted_iota(jnp.int32, (n, n), 0) == lax.broadcasted_iota(jnp.int32, (n, n), 1)
    return jnp.sum(jnp.where(eye, col, 0), axis=0, keepdims=True)


def as_col(row):
    n = row.shape[1]
    eye = lax.broadcasted_iota(jnp.int32, (n, n), 0) == lax.broadcasted_iota(jnp.int32, (n, n), 1)
    return jnp.sum(jnp.where(eye, row, 0), axis=1, keepdims=True)


def kernel(
    nets,
    spans,
    buses,
    groups,
    ptdf_hbm,
    line_dual_hbm,
    cost_hbm,
    demand,
    generation,
    cap,
    storage,
    wear,
    initial,
    leakage,
    line_index,
    rating,
    storage_bus,
    price_in,
    hour_block,
    block_price,
    gen_out,
    storage_out,
    charge_out,
    dual_out,
    price_out,
    ptdf,
    line_dual,
    cost,
    units,
    unit_cols,
    inj,
    inj_other,
    acc,
    pull_own,
    flow_send,
    flow_recv,
    dual_half,
    part_send,
    part_recv,
    limit,
    sums,
    lasts,
    load_sem,
    unit_sem,
    inj_sem,
    part_sem,
    flow_sem,
    dual_sem,
    sum_sem,
    last_sem,
):
    f32, bf16 = jnp.float32, jnp.bfloat16
    me = lax.axis_index("net")
    place = lax.axis_index("tm")
    core = lax.rem(place, 2)
    twin = place + 1 - 2 * core
    hours, nb = demand.shape
    hb = nb // 2
    rows = ptdf.shape[1]
    su = storage.shape[1]
    halves = [
        pl.ds(pl.multiple_of(core * hb, hb), hb),
        pl.ds(pl.multiple_of((1 - core) * hb, hb), hb),
    ]

    def load(j):
        first = pl.multiple_of(peer(me, j, nets) * nb + core * hb, hb)
        return pltpu.make_async_copy(ptdf_hbm.at[:, pl.ds(first, hb)], ptdf.at[j], load_sem.at[j])

    load_dual = pltpu.make_async_copy(line_dual_hbm, line_dual, load_sem.at[nets])
    load_cost = pltpu.make_async_copy(cost_hbm, cost, load_sem.at[nets + 1])
    for j in range(nets):
        load(j).start()
    load_dual.start()
    load_cost.start()

    def device(j, across):
        return {"net": peer(me, j, nets), "tm": twin if across else place}

    barrier = pltpu.get_barrier_semaphore()
    for j in range(1, nets):
        for across in (0, 1):
            pl.semaphore_signal(
                barrier, inc=1, device_id=device(j, across), device_id_type=MESH
            )
    for step in range(1, spans):
        pl.semaphore_signal(
            barrier, inc=1, device_id={"tm": lax.rem(place + step, spans)}, device_id_type=MESH
        )

    units[0, :hours] = storage[...].astype(bf16)
    for h in range(2):
        mine = (generation[:, halves[h]] - demand[:, halves[h]]).astype(bf16)
        if h == 0:
            inj[0, 0, :hours] = mine
        else:
            inj_other[0] = mine
    pl.semaphore_wait(barrier, 2 * (nets - 1) + spans - 1)

    pending = []

    def send(src, dst, sems, slot, target):
        copy = pltpu.make_async_remote_copy(
            src_ref=src,
            dst_ref=dst,
            send_sem=sems.at[0, slot],
            recv_sem=sems.at[1, slot],
            device_id=target,
            device_id_type=MESH,
        )
        copy.start()
        pending.append(copy)
        return copy

    own, other = pl.ds(0, hours), pl.ds(hours, hours)

    def send_injection(turn):
        copies = {}
        copies[0, 1] = send(
            inj_other.at[turn], inj.at[turn, 0, other], inj_sem.at[turn], 1, device(0, 1)
        )
        for j in range(1, nets):
            copies[j, 0] = send(
                inj.at[turn, 0, own], inj.at[turn, j, own], inj_sem.at[turn], 2 * j, device(j, 0)
            )
            copies[j, 1] = send(
                inj_other.at[turn],
                inj.at[turn, j, other],
                inj_sem.at[turn],
                2 * j + 1,
                device(j, 1),
            )
        return copies

    unit_copies = [
        send(units.at[0, own], units.at[j, own], unit_sem, 2 * j, device(j, 0))
        for j in range(1, nets)
    ]
    passed_on = [send(units.at[0, own], units.at[0, other], unit_sem, 1, device(0, 1))]
    inj_copies = send_injection(0)

    index = line_index[...]
    lane, group = lax.rem(index, 128), index // 128
    found = jnp.zeros(index.shape, f32)
    for q in range(rating.shape[0]):
        row = jnp.broadcast_to(rating[q : q + 1, :], index.shape)
        found = jnp.where(
            group == q,
            jnp.take_along_axis(row, lane, axis=1, mode="promise_in_bounds"),
            found,
        )
    limit[...] = found

    unit_part = jnp.sum(storage[...], axis=1, keepdims=True)
    price = as_col(price_in[...])
    block = as_col(hour_block[...])
    kinds = block_price.shape[1]
    hour_price = jnp.sum(
        jnp.where(
            block == lax.broadcasted_iota(jnp.int32, (hours, kinds), 1), block_price[...], 0.0
        ),
        axis=1,
        keepdims=True,
    )

    for j in range(1, nets):
        unit_copies[j - 1].wait_recv()
        passed_on.append(
            send(units.at[j, own], units.at[j, other], unit_sem, 2 * j + 1, device(0, 1))
        )
    for copy in passed_on:
        copy.wait_recv()
    ub = min(256, hb)
    for j in range(nets):
        base = peer(me, j, nets) * nb + core * hb

        def collect(i, c, j=j, base=base):
            bus = base + i * ub + lax.broadcasted_iota(jnp.int32, (ub, su), 0)
            total = jnp.zeros((2 * hours, ub), f32)
            for k in range(nets):
                first = pl.multiple_of(peer(me, k, nets) * su, su)
                hit = jnp.where(storage_bus[:, pl.ds(first, su)] == bus, 1.0, 0.0).astype(bf16)
                total = total + lax.dot_general(units[k], hit, NT, preferred_element_type=f32)
            unit_cols[j, :, pl.ds(pl.multiple_of(i * ub, ub), ub)] = total.astype(bf16)
            return c

        lax.fori_loop(0, hb // ub, collect, 0)

    span_rows = rows // groups
    rb = min(512, span_rows)
    cb = min(512, hb)
    load_dual.wait()
    for turn in range(PASSES):
        old = line_dual if turn == 0 else dual_out
        flow_copies, dual_copies = [], []

        def settle(g):
            flow_copies[g].wait_recv()
            for k in range(span_rows // 128):
                i = g * (span_rows // 128) + k
                r = pl.ds(i * 128, 128)
                bound = limit[i : i + 1, :]
                x = acc[0, :hours, r] + flow_recv[turn, :, r] + old[:, r]
                dual = x - jnp.clip(x, -bound, bound)
                dual_out[:, r] = dual
                dual_half[turn, :hours, r] = dual.astype(bf16)
            r = pl.ds(g * span_rows, span_rows)
            dual_copies.append(
                send(
                    dual_half.at[turn, own, r],
                    dual_half.at[turn, other, r],
                    dual_sem.at[turn],
                    g,
                    device(0, 1),
                )
            )

        for j in range(nets):
            last = j == nets - 1
            if turn == 0:
                load(j).wait()
            if j > 0:
                inj_copies[j, 0].wait_recv()
            inj_copies[j, 1].wait_recv()

            def flow(i, c, j=j, last=last):
                r = pl.ds(pl.multiple_of(i * rb, rb), rb)
                if turn == 0:
                    left = jnp.concatenate([inj[turn, j], unit_cols[j]], axis=0)
                    got = lax.dot_general(left, ptdf[j, r, :], NT, preferred_element_type=f32)
                    unit = got[2 * hours :]
                    got = got[: 2 * hours] + unit
                    if j > 0:
                        unit = unit + acc[1, :, r]
                    acc[1, :, r] = unit
                else:
                    got = lax.dot_general(
                        inj[turn, j], ptdf[j, r, :], NT, preferred_element_type=f32
                    )
                    if j == 0:
                        got = got + acc[1, :, r]
                if j > 0:
                    got = got + acc[0, :, r]
                if last:
                    acc[0, :hours, r] = got[:hours]
                    flow_send[turn, :, r] = got[hours:]
                else:
                    acc[0, :, r] = got
                return c

            if not last:
                lax.fori_loop(0, rows // rb, flow, 0)
        per_group = span_rows // rb
        for g in range(groups + 2):
            if g < groups:
                lax.fori_loop(g * per_group, (g + 1) * per_group, flow, 0)
                r = pl.ds(g * span_rows, span_rows)
                flow_copies.append(
                    send(
                        flow_send.at[turn, :, r],
                        flow_recv.at[turn, :, r],
                        flow_sem.at[turn],
                        g,
                        device(0, 1),
                    )
                )
            if g >= 2:
                settle(g - 2)
        for copy in dual_copies:
            copy.wait_recv()

        part_copies = {}
        for j in list(range(nets - 1, -1, -1)):

            def pull_part(i, c, j=j):
                here = pl.ds(pl.multiple_of(i * cb, cb), cb)
                got = lax.dot_general(
                    dual_half[turn], ptdf[j, :, here], NN, preferred_element_type=f32
                )
                if j > 0:
                    part_send[turn, j, :, here] = got.astype(bf16)
                else:
                    pull_own[:, here] = got[:hours]
                    part_send[turn, j, other, here] = got[hours:].astype(bf16)
                return c

            lax.fori_loop(0, hb // cb, pull_part, 0)
            for h, side in enumerate((own, other)):
                if j or h:
                    part_copies[j, h] = send(
                        part_send.at[turn, j, side],
                        part_recv.at[turn, j, side],
                        part_sem.at[turn],
                        2 * j + h,
                        device(j, h),
                    )
        if turn == 0:
            load_cost.wait()
        gen_old = generation if turn == 0 else gen_out
        part = unit_part
        for j in range(nets - 1, -1, -1):
            for h in range(2):
                if j or h:
                    part_copies[j, h].wait_recv()
        for h, side in enumerate((own, other)):
            pull = pull_own[...] if h == 0 else part_recv[turn, 0, side].astype(f32)
            for j in range(1, nets):
                pull = pull + part_recv[turn, j, side].astype(f32)
            cols = halves[h]
            trial = jnp.clip(
                gen_old[:, cols] - STEP * (cost[:, cols] - price + pull), 0.0, cap[:, cols]
            )
            gen_out[:, cols] = trial
            part = part + jnp.sum(trial - demand[:, cols], axis=1, keepdims=True)
        sums[turn, 0, :, :hours] = jnp.broadcast_to(as_row(part), (8, hours))
        sum_copies = [
            send(sums.at[turn, 0], sums.at[turn, j], sum_sem.at[turn], j, device(j, 0))
            for j in range(1, nets)
        ]
        whole = sums[turn, 0]
        for j in range(1, nets):
            sum_copies[j - 1].wait_recv()
            whole = whole + sums[turn, j]
        mismatch = as_col(whole[0:1, :hours])
        price = price - BAL * mismatch / buses
        for h in range(2):
            gen = gen_out[:, halves[h]] - mismatch / buses
            gen_out[:, halves[h]] = gen
            if turn + 1 < PASSES:
                mine = (gen - demand[:, halves[h]]).astype(bf16)
                if h == 0:
                    inj[turn + 1, 0, :hours] = mine
                else:
                    inj_other[turn + 1] = mine
        if turn + 1 < PASSES:
            inj_copies = send_injection(turn + 1)

    stored = storage[...]
    stored = jnp.clip(
        stored + STEP_UNIT * (price + hour_price - wear[...] * stored), -1.0, 1.0
    )
    storage_out[...] = stored
    keep = 1.0 - leakage[...]
    running = -ETA * stored
    hour = lax.broadcasted_iota(jnp.int32, (hours, su), 0)
    growth = jnp.ones((hours, su), f32)
    factor = keep
    span = 1
    while span < hours:
        moved = jnp.where(hour >= span, pltpu.roll(running, span, axis=0), 0.0)
        running = running + factor * moved
        growth = jnp.where(lax.rem((hour + 1) // span, 2) == 1, growth * factor, growth)
        factor = factor * factor
        span = span * 2
    while span <= hours:
        growth = jnp.where(lax.rem((hour + 1) // span, 2) == 1, growth * factor, growth)
        factor = factor * factor
        span = span * 2
    lasts[0] = jnp.broadcast_to(running[hours - 1 :, :], (8, su))
    last_copies = [
        send(lasts.at[0], lasts.at[s], last_sem, s, {"tm": lax.rem(place + s, spans)})
        for s in range(1, spans)
    ]
    price_out[...] = as_row(price)
    block_keep = growth[hours - 1 :, :]
    for copy in last_copies:
        copy.wait_recv()
    entering = initial[...]
    for s in range(spans - 1, 0, -1):
        entering = jnp.where(s <= place, block_keep * entering + lasts[s, 0:1, :], entering)
    charge_out[...] = growth * entering + running
    for copy in pending:
        copy.wait_send()


def write_out(*refs):
    count = len(refs) // 2
    for source, target in zip(refs[:count], refs[count:]):
        target[...] = source[...]


def per_device(
    ptdf,
    demand,
    generation,
    cost,
    gen_cap,
    storage,
    wear,
    initial_charge,
    leakage,
    line_dual,
    line_index,
    rating,
    storage_bus,
    balance_dual,
    hour_block,
    block_price,
):
    nets, spans = lax.axis_size("net"), lax.axis_size("tm")
    rows, _ = ptdf.shape
    nb, hours = demand.shape
    su = storage.shape[0]
    buses, hb = nb * nets, nb // 2
    groups = 4 if rows % 512 == 0 else 1
    f32, bf16 = jnp.float32, jnp.bfloat16
    vmem = pl.BlockSpec(memory_space=pltpu.VMEM)
    hbm = pl.BlockSpec(memory_space=pl.ANY)
    sem = pltpu.SemaphoreType.DMA
    out_shape = (
        jax.ShapeDtypeStruct((hours, nb), f32),
        jax.ShapeDtypeStruct((hours, su), f32),
        jax.ShapeDtypeStruct((hours, su), f32),
        jax.ShapeDtypeStruct((hours, rows), f32),
        jax.ShapeDtypeStruct((1, hours), f32),
    )
    found = pl.pallas_call(
        functools.partial(kernel, nets, spans, buses, groups),
        out_shape=out_shape,
        in_specs=[hbm] * 3 + [vmem] * 13,
        out_specs=(vmem,) * 5,
        scratch_shapes=[
            pltpu.VMEM((nets, rows, hb), bf16),
            pltpu.VMEM((hours, rows), f32),
            pltpu.VMEM((hours, nb), f32),
            pltpu.VMEM((nets, 2 * hours, su), bf16),
            pltpu.VMEM((nets, 2 * hours, hb), bf16),
            pltpu.VMEM((PASSES, nets, 2 * hours, hb), bf16),
            pltpu.VMEM((PASSES, hours, hb), bf16),
            pltpu.VMEM((2, 2 * hours, rows), f32),
            pltpu.VMEM((hours, hb), f32),
            pltpu.VMEM((PASSES, hours, rows), f32),
            pltpu.VMEM((PASSES, hours, rows), f32),
            pltpu.VMEM((PASSES, 2 * hours, rows), bf16),
            pltpu.VMEM((PASSES, nets, 2 * hours, hb), bf16),
            pltpu.VMEM((PASSES, nets, 2 * hours, hb), bf16),
            pltpu.VMEM((rows // 128, 128), f32),
            pltpu.VMEM((PASSES, nets, 8, 128), f32),
            pltpu.VMEM((spans, 8, su), f32),
            sem((nets + 2,)),
            sem((2, 2 * nets)),
            sem((PASSES, 2, 2 * nets)),
            sem((PASSES, 2, 2 * nets)),
            sem((PASSES, 2, groups)),
            sem((PASSES, 2, groups)),
            sem((PASSES, 2, nets)),
            sem((2, spans)),
        ],
        compiler_params=pltpu.CompilerParams(
            collective_id=0, has_side_effects=True, vmem_limit_bytes=64 * 1000 * 1000
        ),
    )(
        ptdf,
        line_dual.T,
        cost.T,
        demand.T,
        generation.T,
        gen_cap[None, :],
        storage.T,
        wear[None, :],
        initial_charge[None, :],
        leakage[None, :],
        line_index.reshape(-1, 128),
        rating.reshape(-1, 128),
        storage_bus[None, :],
        balance_dual[None, :],
        hour_block[None, :],
        block_price[None, :],
    )
    gen, stored, charge, dual, price = pl.pallas_call(
        write_out,
        out_shape=out_shape,
        in_specs=[vmem] * 5,
        out_specs=(vmem,) * 5,
        compiler_params=pltpu.CompilerParams(vmem_limit_bytes=8 * 2**20),
    )(*found)
    return (gen.T, stored.T, charge.T, dual.T, price[0])


def solution(mesh):
    in_specs = (
        P("net", None),
        P("net", "tm"),
        P("net", "tm"),
        P("net", "tm"),
        P("net"),
        P("net", "tm"),
        P("net"),
        P("net"),
        P("net"),
        P("net", "tm"),
        P("net"),
        P(),
        P(),
        P("tm"),
        P("tm"),
        P(),
    )
    out_specs = (P("net", "tm"), P("net", "tm"), P("net", "tm"), P("net", "tm"), P("tm"))
    return jax.shard_map(
        per_device, mesh=mesh, in_specs=in_specs, out_specs=out_specs, check_vma=False
    )
```

```python
import functools

import jax
import jax.numpy as jnp
from jax import lax
from jax.experimental import pallas as pl
from jax.experimental.pallas import tpu as pltpu
from jax.sharding import PartitionSpec as P

PASSES = 2
STEP = 0.1
BAL = 0.5
STEP_UNIT = 0.2
ETA = 0.0625
MESH = pl.DeviceIdType.MESH
NT = (((1,), (1,)), ((), ()))
NN = (((1,), (0,)), ((), ()))


def peer(me, step, count):
    other, bit = 0, 1
    while bit < count:
        mine = lax.rem(me // bit, 2)
        other = other + bit * ((1 - mine) if step & bit else mine)
        bit *= 2
    return other


def as_row(col):
    n = col.shape[0]
    eye = lax.broadcasted_iota(jnp.int32, (n, n), 0) == lax.broadcasted_iota(jnp.int32, (n, n), 1)
    return jnp.sum(jnp.where(eye, col, 0), axis=0, keepdims=True)


def as_col(row):
    n = row.shape[1]
    eye = lax.broadcasted_iota(jnp.int32, (n, n), 0) == lax.broadcasted_iota(jnp.int32, (n, n), 1)
    return jnp.sum(jnp.where(eye, row, 0), axis=1, keepdims=True)


def kernel(
    nets,
    spans,
    buses,
    groups,
    ptdf_hbm,
    line_dual_hbm,
    cost_hbm,
    demand,
    generation,
    cap,
    storage,
    wear,
    initial,
    leakage,
    line_index,
    rating,
    storage_bus,
    price_in,
    hour_block,
    block_price,
    gen_out,
    storage_out,
    charge_out,
    dual_out,
    price_out,
    ptdf,
    line_dual,
    cost,
    units,
    unit_cols,
    inj,
    inj_other,
    acc,
    pull_own,
    flow_send,
    flow_recv,
    dual_half,
    part_send,
    part_recv,
    limit,
    sums,
    lasts,
    load_sem,
    unit_sem,
    inj_sem,
    part_sem,
    flow_sem,
    dual_sem,
    sum_sem,
    last_sem,
):
    f32, bf16 = jnp.float32, jnp.bfloat16
    me = lax.axis_index("net")
    place = lax.axis_index("tm")
    core = lax.rem(place, 2)
    twin = place + 1 - 2 * core
    hours, nb = demand.shape
    hb = nb // 2
    rows = ptdf.shape[1]
    su = storage.shape[1]
    halves = [
        pl.ds(pl.multiple_of(core * hb, hb), hb),
        pl.ds(pl.multiple_of((1 - core) * hb, hb), hb),
    ]

    def load(j):
        first = pl.multiple_of(peer(me, j, nets) * nb + core * hb, hb)
        return pltpu.make_async_copy(ptdf_hbm.at[:, pl.ds(first, hb)], ptdf.at[j], load_sem.at[j])

    load_dual = pltpu.make_async_copy(line_dual_hbm, line_dual, load_sem.at[nets])
    load_cost = pltpu.make_async_copy(cost_hbm, cost, load_sem.at[nets + 1])
    for j in range(nets):
        load(j).start()
    load_dual.start()
    load_cost.start()

    def device(j, across):
        return {"net": peer(me, j, nets), "tm": twin if across else place}

    barrier = pltpu.get_barrier_semaphore()
    for j in range(1, nets):
        for across in (0, 1):
            pl.semaphore_signal(
                barrier, inc=1, device_id=device(j, across), device_id_type=MESH
            )
    for step in range(1, spans):
        pl.semaphore_signal(
            barrier, inc=1, device_id={"tm": lax.rem(place + step, spans)}, device_id_type=MESH
        )

    units[0, :hours] = storage[...].astype(bf16)
    for h in range(2):
        mine = (generation[:, halves[h]] - demand[:, halves[h]]).astype(bf16)
        if h == 0:
            inj[0, 0, :hours] = mine
        else:
            inj_other[0] = mine
    pl.semaphore_wait(barrier, 2 * (nets - 1) + spans - 1)

    pending = []

    def send(src, dst, sems, slot, target):
        copy = pltpu.make_async_remote_copy(
            src_ref=src,
            dst_ref=dst,
            send_sem=sems.at[0, slot],
            recv_sem=sems.at[1, slot],
            device_id=target,
            device_id_type=MESH,
        )
        copy.start()
        pending.append(copy)
        return copy

    own, other = pl.ds(0, hours), pl.ds(hours, hours)

    def send_injection(turn):
        copies = {}
        copies[0, 1] = send(
            inj_other.at[turn], inj.at[turn, 0, other], inj_sem.at[turn], 1, device(0, 1)
        )
        for j in range(1, nets):
            copies[j, 0] = send(
                inj.at[turn, 0, own], inj.at[turn, j, own], inj_sem.at[turn], 2 * j, device(j, 0)
            )
            copies[j, 1] = send(
                inj_other.at[turn],
                inj.at[turn, j, other],
                inj_sem.at[turn],
                2 * j + 1,
                device(j, 1),
            )
        return copies

    unit_copies = [
        send(units.at[0, own], units.at[j, own], unit_sem, 2 * j, device(j, 0))
        for j in range(1, nets)
    ]
    passed_on = [send(units.at[0, own], units.at[0, other], unit_sem, 1, device(0, 1))]
    inj_copies = send_injection(0)

    index = line_index[...]
    lane, group = lax.rem(index, 128), index // 128
    found = jnp.zeros(index.shape, f32)
    for q in range(rating.shape[0]):
        row = jnp.broadcast_to(rating[q : q + 1, :], index.shape)
        found = jnp.where(
            group == q,
            jnp.take_along_axis(row, lane, axis=1, mode="promise_in_bounds"),
            found,
        )
    limit[...] = found

    unit_part = jnp.sum(storage[...], axis=1, keepdims=True)
    price = as_col(price_in[...])
    block = as_col(hour_block[...])
    kinds = block_price.shape[1]
    hour_price = jnp.sum(
        jnp.where(
            block == lax.broadcasted_iota(jnp.int32, (hours, kinds), 1), block_price[...], 0.0
        ),
        axis=1,
        keepdims=True,
    )

    for j in range(1, nets):
        unit_copies[j - 1].wait_recv()
        passed_on.append(
            send(units.at[j, own], units.at[j, other], unit_sem, 2 * j + 1, device(0, 1))
        )
    for copy in passed_on:
        copy.wait_recv()
    ub = min(512, hb)
    for j in range(nets):
        base = peer(me, j, nets) * nb + core * hb

        def collect(i, c, j=j, base=base):
            bus = base + i * ub + lax.broadcasted_iota(jnp.int32, (ub, su), 0)
            total = jnp.zeros((2 * hours, ub), f32)
            for k in range(nets):
                first = pl.multiple_of(peer(me, k, nets) * su, su)
                hit = jnp.where(storage_bus[:, pl.ds(first, su)] == bus, 1.0, 0.0).astype(bf16)
                total = total + lax.dot_general(units[k], hit, NT, preferred_element_type=f32)
            unit_cols[j, :, pl.ds(pl.multiple_of(i * ub, ub), ub)] = total.astype(bf16)
            return c

        lax.fori_loop(0, hb // ub, collect, 0)

    span_rows = rows // groups
    rb = 2048 if rows % 2048 == 0 else span_rows
    cb = min(512, hb)
    load_dual.wait()
    for turn in range(PASSES):
        old = line_dual if turn == 0 else dual_out
        flow_copies, dual_copies = [], []

        def settle(g):
            flow_copies[g].wait_recv()
            for k in range(span_rows // 128):
                i = g * (span_rows // 128) + k
                r = pl.ds(i * 128, 128)
                bound = limit[i : i + 1, :]
                x = acc[0, :hours, r] + flow_recv[turn, :, r] + old[:, r]
                dual = x - jnp.clip(x, -bound, bound)
                dual_out[:, r] = dual
                dual_half[turn, :hours, r] = dual.astype(bf16)
            r = pl.ds(g * span_rows, span_rows)
            dual_copies.append(
                send(
                    dual_half.at[turn, own, r],
                    dual_half.at[turn, other, r],
                    dual_sem.at[turn],
                    g,
                    device(0, 1),
                )
            )

        for j in range(nets):
            last = j == nets - 1
            if turn == 0:
                load(j).wait()
            if j > 0:
                inj_copies[j, 0].wait_recv()
            inj_copies[j, 1].wait_recv()

            def flow(i, c, j=j, last=last):
                size = span_rows if last else rb
                r = pl.ds(pl.multiple_of(i * size, size), size)
                if turn == 0:
                    left = jnp.concatenate([inj[turn, j], unit_cols[j]], axis=0)
                    got = lax.dot_general(left, ptdf[j, r, :], NT, preferred_element_type=f32)
                    unit = got[2 * hours :]
                    got = got[: 2 * hours] + unit
                    if j > 0:
                        unit = unit + acc[1, :, r]
                    acc[1, :, r] = unit
                else:
                    got = lax.dot_general(
                        inj[turn, j], ptdf[j, r, :], NT, preferred_element_type=f32
                    )
                    if j == 0:
                        got = got + acc[1, :, r]
                if j > 0:
                    got = got + acc[0, :, r]
                if last:
                    acc[0, :hours, r] = got[:hours]
                    flow_send[turn, :, r] = got[hours:]
                else:
                    acc[0, :, r] = got
                return c

            if not last:
                lax.fori_loop(0, rows // rb, flow, 0)
        for g in range(groups + 2):
            if g < groups:
                lax.fori_loop(g, g + 1, flow, 0)
                r = pl.ds(g * span_rows, span_rows)
                flow_copies.append(
                    send(
                        flow_send.at[turn, :, r],
                        flow_recv.at[turn, :, r],
                        flow_sem.at[turn],
                        g,
                        device(0, 1),
                    )
                )
            if g >= 2:
                settle(g - 2)
        for copy in dual_copies:
            copy.wait_recv()

        part_copies = {}
        for j in list(range(nets - 1, -1, -1)):

            def pull_part(i, c, j=j):
                here = pl.ds(pl.multiple_of(i * cb, cb), cb)
                got = lax.dot_general(
                    dual_half[turn], ptdf[j, :, here], NN, preferred_element_type=f32
                )
                if j > 0:
                    part_send[turn, j, :, here] = got.astype(bf16)
                else:
                    pull_own[:, here] = got[:hours]
                    part_send[turn, j, other, here] = got[hours:].astype(bf16)
                return c

            lax.fori_loop(0, hb // cb, pull_part, 0)
            for h, side in enumerate((own, other)):
                if j or h:
                    part_copies[j, h] = send(
                        part_send.at[turn, j, side],
                        part_recv.at[turn, j, side],
                        part_sem.at[turn],
                        2 * j + h,
                        device(j, h),
                    )
        if turn == 0:
            load_cost.wait()
        gen_old = generation if turn == 0 else gen_out
        part = unit_part
        for j in range(nets - 1, -1, -1):
            for h in range(2):
                if j or h:
                    part_copies[j, h].wait_recv()
        for h, side in enumerate((own, other)):
            pull = pull_own[...] if h == 0 else part_recv[turn, 0, side].astype(f32)
            for j in range(1, nets):
                pull = pull + part_recv[turn, j, side].astype(f32)
            cols = halves[h]
            trial = jnp.clip(
                gen_old[:, cols] - STEP * (cost[:, cols] - price + pull), 0.0, cap[:, cols]
            )
            gen_out[:, cols] = trial
            part = part + jnp.sum(trial - demand[:, cols], axis=1, keepdims=True)
        sums[turn, 0, :, :hours] = jnp.broadcast_to(as_row(part), (8, hours))
        sum_copies = [
            send(sums.at[turn, 0], sums.at[turn, j], sum_sem.at[turn], j, device(j, 0))
            for j in range(1, nets)
        ]
        whole = sums[turn, 0]
        for j in range(1, nets):
            sum_copies[j - 1].wait_recv()
            whole = whole + sums[turn, j]
        mismatch = as_col(whole[0:1, :hours])
        price = price - BAL * mismatch / buses
        for h in range(2):
            gen = gen_out[:, halves[h]] - mismatch / buses
            gen_out[:, halves[h]] = gen
            if turn + 1 < PASSES:
                mine = (gen - demand[:, halves[h]]).astype(bf16)
                if h == 0:
                    inj[turn + 1, 0, :hours] = mine
                else:
                    inj_other[turn + 1] = mine
        if turn + 1 < PASSES:
            inj_copies = send_injection(turn + 1)

    stored = storage[...]
    stored = jnp.clip(
        stored + STEP_UNIT * (price + hour_price - wear[...] * stored), -1.0, 1.0
    )
    storage_out[...] = stored
    keep = 1.0 - leakage[...]
    running = -ETA * stored
    hour = lax.broadcasted_iota(jnp.int32, (hours, su), 0)
    growth = jnp.ones((hours, su), f32)
    factor = keep
    span = 1
    while span < hours:
        moved = jnp.where(hour >= span, pltpu.roll(running, span, axis=0), 0.0)
        running = running + factor * moved
        growth = jnp.where(lax.rem((hour + 1) // span, 2) == 1, growth * factor, growth)
        factor = factor * factor
        span = span * 2
    while span <= hours:
        growth = jnp.where(lax.rem((hour + 1) // span, 2) == 1, growth * factor, growth)
        factor = factor * factor
        span = span * 2
    lasts[0] = jnp.broadcast_to(running[hours - 1 :, :], (8, su))
    last_copies = [
        send(lasts.at[0], lasts.at[s], last_sem, s, {"tm": lax.rem(place + s, spans)})
        for s in range(1, spans)
    ]
    price_out[...] = as_row(price)
    block_keep = growth[hours - 1 :, :]
    for copy in last_copies:
        copy.wait_recv()
    entering = initial[...]
    for s in range(spans - 1, 0, -1):
        entering = jnp.where(s <= place, block_keep * entering + lasts[s, 0:1, :], entering)
    charge_out[...] = growth * entering + running
    for copy in pending:
        copy.wait_send()


def write_out(*refs):
    count = len(refs) // 2
    for source, target in zip(refs[:count], refs[count:]):
        target[...] = source[...]


def per_device(
    ptdf,
    demand,
    generation,
    cost,
    gen_cap,
    storage,
    wear,
    initial_charge,
    leakage,
    line_dual,
    line_index,
    rating,
    storage_bus,
    balance_dual,
    hour_block,
    block_price,
):
    nets, spans = lax.axis_size("net"), lax.axis_size("tm")
    rows, _ = ptdf.shape
    nb, hours = demand.shape
    su = storage.shape[0]
    buses, hb = nb * nets, nb // 2
    groups = 4 if rows % 512 == 0 else 1
    f32, bf16 = jnp.float32, jnp.bfloat16
    vmem = pl.BlockSpec(memory_space=pltpu.VMEM)
    hbm = pl.BlockSpec(memory_space=pl.ANY)
    sem = pltpu.SemaphoreType.DMA
    out_shape = (
        jax.ShapeDtypeStruct((hours, nb), f32),
        jax.ShapeDtypeStruct((hours, su), f32),
        jax.ShapeDtypeStruct((hours, su), f32),
        jax.ShapeDtypeStruct((hours, rows), f32),
        jax.ShapeDtypeStruct((1, hours), f32),
    )
    found = pl.pallas_call(
        functools.partial(kernel, nets, spans, buses, groups),
        out_shape=out_shape,
        in_specs=[hbm] * 3 + [vmem] * 13,
        out_specs=(vmem,) * 5,
        scratch_shapes=[
            pltpu.VMEM((nets, rows, hb), bf16),
            pltpu.VMEM((hours, rows), f32),
            pltpu.VMEM((hours, nb), f32),
            pltpu.VMEM((nets, 2 * hours, su), bf16),
            pltpu.VMEM((nets, 2 * hours, hb), bf16),
            pltpu.VMEM((PASSES, nets, 2 * hours, hb), bf16),
            pltpu.VMEM((PASSES, hours, hb), bf16),
            pltpu.VMEM((2, 2 * hours, rows), f32),
            pltpu.VMEM((hours, hb), f32),
            pltpu.VMEM((PASSES, hours, rows), f32),
            pltpu.VMEM((PASSES, hours, rows), f32),
            pltpu.VMEM((PASSES, 2 * hours, rows), bf16),
            pltpu.VMEM((PASSES, nets, 2 * hours, hb), bf16),
            pltpu.VMEM((PASSES, nets, 2 * hours, hb), bf16),
            pltpu.VMEM((rows // 128, 128), f32),
            pltpu.VMEM((PASSES, nets, 8, 128), f32),
            pltpu.VMEM((spans, 8, su), f32),
            sem((nets + 2,)),
            sem((2, 2 * nets)),
            sem((PASSES, 2, 2 * nets)),
            sem((PASSES, 2, 2 * nets)),
            sem((PASSES, 2, groups)),
            sem((PASSES, 2, groups)),
            sem((PASSES, 2, nets)),
            sem((2, spans)),
        ],
        compiler_params=pltpu.CompilerParams(
            collective_id=0, has_side_effects=True, vmem_limit_bytes=64 * 1000 * 1000
        ),
    )(
        ptdf,
        line_dual.T,
        cost.T,
        demand.T,
        generation.T,
        gen_cap[None, :],
        storage.T,
        wear[None, :],
        initial_charge[None, :],
        leakage[None, :],
        line_index.reshape(-1, 128),
        rating.reshape(-1, 128),
        storage_bus[None, :],
        balance_dual[None, :],
        hour_block[None, :],
        block_price[None, :],
    )
    gen, stored, charge, dual, price = pl.pallas_call(
        write_out,
        out_shape=out_shape,
        in_specs=[vmem] * 5,
        out_specs=(vmem,) * 5,
        compiler_params=pltpu.CompilerParams(vmem_limit_bytes=64 * 1000 * 1000),
    )(*found)
    return (gen.T, stored.T, charge.T, dual.T, price[0])


def solution(mesh):
    in_specs = (
        P("net", None),
        P("net", "tm"),
        P("net", "tm"),
        P("net", "tm"),
        P("net"),
        P("net", "tm"),
        P("net"),
        P("net"),
        P("net"),
        P("net", "tm"),
        P("net"),
        P(),
        P(),
        P("tm"),
        P("tm"),
        P(),
    )
    out_specs = (P("net", "tm"), P("net", "tm"), P("net", "tm"), P("net", "tm"), P("tm"))
    return jax.shard_map(
        per_device, mesh=mesh, in_specs=in_specs, out_specs=out_specs, check_vma=False
    )
```
